32 devices in a mesh: grp: 2 (over y), tok: 4 (over z), feat: 4 (over x, core).
Axes of the slice: x: 2, y: 2, z: 4, core: 2. Of those that a mesh axis runs over, the one named last changes fastest.
Arguments:
- acts: bfloat16 [6144, 28672], P(('grp', 'tok'), 'feat'), parts along dimension 0, may hold values from -6 to 6
- grads: bfloat16 [6144, 8192], P(('grp', 'tok'), 'feat'), parts along dimension 0, may hold values from -6 to 6
- proj_in: bfloat16 [28672, 512], P('feat'), may hold values from -0.03125 to 0.03125
- proj_out: bfloat16 [8192, 512], P('feat'), may hold values from -0.0625 to 0.0625
- doc_lengths: int32 [8], P('grp'), parts along dimension 0, may hold values from 1 to 1536, 3072 in all
- doc_owner: int32 [8], P('grp'), parts along dimension 0, may hold values from 0 to 3, as said below
Outputs:
- doc_grads: float32 [8, 512, 512], P(('grp', 'tok'), 'feat'), parts along dimension 0
The draws below stay inside these ranges and needn't reach their ends.
There are 2 independent parts, one for each index of `grp`. The reference program is written for one: setup_inputs(seed, part) draws one part's arguments, and reference() takes and returns one part's arrays. A program takes and returns all parts, laid end to end along the dimension named above; an argument that names none is the same for every part. Nothing has to cross between parts.
Inputs may be any that keep to these rules, and one draw needn't show every extreme that they name: `doc_lengths`: the lengths sum to 3072; the largest is exactly 1536. `doc_owner`: every index along tok owns exactly 1 documents.
All inputs are finite; a program needn't handle non-finite values.
Results may differ from the reference program's by a relative error of at most 0.0043.
Values may be sent and summed in bfloat16 or wider, within the bound.
A program may use at most 64 MiB of HBM per device.

```python
import math
import jax
import jax.numpy as jnp
import numpy as np
from jax import lax

DIN = 28672
DOUT = 8192
RANK = 512
DOC_SLOTS = 1
TOKENS = 3072
DOCS = 4
LEN_MOST = 1536


def draw_doc_owner(key, part):
    shuffled = jax.random.permutation(jax.random.fold_in(key, 11), DOCS)
    return (shuffled // DOC_SLOTS).astype(jnp.int32)


def shard_levels(rng, extent, shards, low, high):
    def one(dim, shards_of):
        heights = jax.random.uniform(jax.random.fold_in(jax.random.fold_in(rng, 6), dim), (shards_of,), jnp.float32, low / len(shards), high / len(shards))
        return jnp.repeat(jnp.exp(heights), extent[dim] // shards_of).reshape((-1,) + (1,) * (len(extent) - dim - 1))

    level = one(*shards[0])
    for cut in shards[1:]:
        level = level * one(*cut)
    return level


def split_up(amount, total, reach, lean):
    weights = [(1 << 20) // math.isqrt(rank ** lean) + 1 for rank in range(2, amount + 1)]
    spare, holding = total - reach - (amount - 1), [1] * (amount - 1)
    while spare > 0:
        movable = [i for i in range(amount - 1) if holding[i] < reach]
        whole, remaining = sum([weights[i] for i in movable]), spare
        for i in movable:
            addition = min(reach - holding[i], max(1, remaining * weights[i] // whole), spare)
            holding[i] = holding[i] + addition
            spare = spare - addition
    return np.array([reach] + holding)


def ragged_sizes(own_key, number_of, total, reach, lean):
    if number_of == 2:
        one = jax.random.randint(own_key, (), max(1, total - reach), min(reach, total - 1) + 1)
        return jnp.stack([one, total - one])
    lengths = jnp.asarray(split_up(number_of, total, reach, lean), jnp.int32)
    couples = (number_of - 1) // 2
    giver, taker = lengths[1:1 + 2 * couples:2], lengths[2:2 + 2 * couples:2]
    slack = jnp.minimum(giver - 1, reach - taker)
    shifted = jax.random.randint(jax.random.fold_in(own_key, 1), (couples,), 0, 1 << 20) % (slack + 1)
    lengths = lengths.at[1:1 + 2 * couples:2].set(giver - shifted).at[2:2 + 2 * couples:2].set(taker + shifted)
    return lengths[jax.random.permutation(jax.random.fold_in(own_key, 2), number_of)]


def centred(own_key, dims, width, reach, split=(), held_as=jnp.bfloat16):
    entries = jax.random.normal(own_key, dims, jnp.float32) * width
    if len(split) > 0:
        entries = shard_levels(own_key, dims, split, -0.22, 0.18) * entries
    return jnp.clip(entries, min=-reach, max=reach).astype(held_as)


def setup_inputs(seed: int = 0, part: int = 0) -> dict:
    key_of = jax.random.split(jax.random.key(seed), 7)
    own_keys = jax.random.split(jax.random.fold_in(key_of[6], part), 7)
    return {
        "acts": centred(own_keys[0], (TOKENS, DIN), 1.0, 6.0, ((0, 4), (1, 4))),
        "grads": centred(own_keys[1], (TOKENS, DOUT), 1.0, 6.0, ((0, 4), (1, 4))),
        "proj_in": centred(key_of[2], (DIN, RANK), DIN ** -0.5, 0.03125, ((0, 4),)),
        "proj_out": centred(key_of[3], (DOUT, RANK), DOUT ** -0.5, 0.0625, ((0, 4),)),
        "doc_lengths": ragged_sizes(own_keys[4], DOCS, TOKENS, LEN_MOST, 2).astype(jnp.int32),
        "doc_owner": draw_doc_owner(jax.random.fold_in(jax.random.fold_in(key_of[6], part), 71), part),
    }


def reference(acts, grads, proj_in, proj_out, doc_lengths, doc_owner):
    inputs_low = jnp.dot(acts, proj_in, preferred_element_type=jnp.float32).astype(jnp.bfloat16)
    grads_low = jnp.dot(grads, proj_out, preferred_element_type=jnp.float32).astype(jnp.bfloat16)
    doc_ends = jnp.cumsum(doc_lengths).astype(jnp.int32)
    doc_starts = (doc_ends - doc_lengths).astype(jnp.int32)
    position = jnp.arange(acts.shape[0], dtype=jnp.int32)

    def one_doc(bounds):
        start_at, end_at = bounds
        member = ((position >= start_at) & (position < end_at)).astype(grads_low.dtype)
        weighted = grads_low * member[:, None]
        return jnp.dot(weighted.T, inputs_low, preferred_element_type=jnp.float32)
    gradients = lax.map(one_doc, (doc_starts, doc_ends))
    gradients = gradients * lax.rsqrt(doc_lengths.astype(jnp.float32))[:, None, None]
    doc_index = jnp.arange(doc_owner.shape[0], dtype=jnp.int32)
    same_owner = doc_owner[:, None] == doc_owner[None, :]
    earlier = doc_index[:, None] < doc_index[None, :]
    slot_rank = lax.optimization_barrier(jnp.sum((same_owner & earlier).astype(jnp.int32), axis=0)).astype(jnp.int32)
    target = (doc_owner * DOC_SLOTS + slot_rank).astype(jnp.int32)
    return jnp.zeros_like(gradients).at[target].set(gradients)
```

```python
import functools
import jax
import jax.numpy as jnp
from jax import lax
from jax.experimental import pallas as pl
from jax.experimental.pallas import tpu as pltpu
from jax.sharding import PartitionSpec as P

MESH = pl.DeviceIdType.MESH
CORES = 2
HALVES = 2
OUT_STEPS = 2
IN_STEPS = 4


def kernel(
    toks, feats, len_ref, own_ref, acts_hbm, grads_hbm, pin_hbm, pout_hbm, res_ref,
    acts, grads, pin, pout,
    gp, gr, gown, gxs, gxr, gt, gm,
    ip, ir, isum, ixs, ixr, il, zf, zs, zr,
    a_sem, g_sem, pi_sem, po_sem,
    gs_send, gs_recv, gx_send, gx_recv, is_send, is_recv, ix_send, ix_recv,
    ig_send, ig_recv, z_send, z_recv,
):
    z = lax.axis_index("tok")
    f = lax.axis_index("feat")
    chips = feats // CORES
    x, c = f // CORES, lax.rem(f, CORES)
    oc = 1 - c
    sib = {"feat": x * CORES + oc}
    docs = len_ref.shape[0]
    slots = docs // toks
    rows, din = acts.shape
    dout = grads.shape[1]
    half = rows // HALVES
    width = gown.shape[2]
    rank = pin.shape[1]
    cols = rank // HALVES
    kin, kout = din // IN_STEPS, dout // OUT_STEPS

    def chip(dx):
        return lax.rem(x + dx, chips)

    def at_x(dx):
        return {"feat": chip(dx) * CORES + c}

    def tok(dz):
        return lax.rem(z + dz, toks)

    def g_copy(j):
        return (
            pltpu.make_async_copy(
                grads_hbm.at[:, pl.ds(j * kout, kout)], grads.at[:, pl.ds(j * kout, kout)], g_sem.at[j]
            ),
            pltpu.make_async_copy(
                pout_hbm.at[pl.ds(j * kout, kout)], pout.at[pl.ds(j * kout, kout)], po_sem.at[j]
            ),
        )

    def a_copy(r, j):
        return pltpu.make_async_copy(
            acts_hbm.at[pl.ds(r * half, half), pl.ds(j * kin, kin)],
            acts.at[pl.ds(r * half, half), pl.ds(j * kin, kin)],
            a_sem.at[r, j],
        )

    def p_copy(k, j):
        return pltpu.make_async_copy(
            pin_hbm.at[pl.ds(j * kin, kin), pl.ds(k * cols, cols)],
            pin.at[pl.ds(j * kin, kin), pl.ds(k * cols, cols)],
            pi_sem.at[k, j],
        )

    barrier = pltpu.get_barrier_semaphore()
    peers = [sib] + [at_x(dx) for dx in range(1, chips)] + [{"tok": tok(dz)} for dz in range(1, toks)]
    for peer in peers:
        pl.semaphore_signal(barrier, inc=1, device_id=peer, device_id_type=MESH)

    for j in range(OUT_STEPS):
        for copy in g_copy(j):
            copy.start()
    for j in range(IN_STEPS):
        p_copy(0, j).start()
        a_copy(0, j).start()
    for r in range(1, HALVES):
        for j in range(IN_STEPS):
            a_copy(r, j).start()
    for k in range(1, HALVES):
        for j in range(IN_STEPS):
            p_copy(k, j).start()

    def remote(src, dst, send, recv, device):
        return pltpu.make_async_remote_copy(
            src_ref=src, dst_ref=dst, send_sem=send, recv_sem=recv, device_id=device, device_id_type=MESH
        )

    def g_sib(h):
        return remote(gp.at[oc, h], gr.at[h], gs_send.at[h], gs_recv.at[h], sib)

    def g_x(h, dx):
        return remote(gxs.at[h, dx - 1], gxr.at[h, dx - 1], gx_send.at[h, dx - 1], gx_recv.at[h, dx - 1], at_x(dx))

    def i_sib(u):
        return remote(ip.at[u, oc], ir.at[u], is_send.at[u], is_recv.at[u], sib)

    def i_x(u, dx):
        return remote(ixs.at[u], ixr.at[u, dx - 1], ix_send.at[u, dx - 1], ix_recv.at[u, dx - 1], at_x(dx))

    def i_gather(u):
        place = il.at[u // HALVES, u % HALVES, c]
        return remote(place, place, ig_send.at[u], ig_recv.at[u], sib)

    def z_copy(k, dz):
        return remote(
            zs.at[k, tok(dz)], zr.at[k, dz - 1], z_send.at[k, dz - 1], z_recv.at[k, dz - 1], {"tok": tok(dz)}
        )

    def g_matmul(h):
        total = None
        for j in range(OUT_STEPS):
            if h == 0:
                for copy in g_copy(j):
                    copy.wait()
            term = jnp.dot(
                grads[h * half : (h + 1) * half, j * kout : (j + 1) * kout],
                pout[j * kout : (j + 1) * kout, :],
                preferred_element_type=jnp.float32,
            )
            total = term if total is None else total + term
        for b in range(feats):
            gp[b % CORES, h, b // CORES] = total[:, b * width : (b + 1) * width]

    def g_share(h):
        g_sib(h).wait_recv()
        gown[h] = gp[c, h, x] + gr[h, x]
        for dx in range(1, chips):
            gxs[h, dx - 1] = (gp[c, h, chip(dx)] + gr[h, chip(dx)]).astype(jnp.bfloat16)
            g_x(h, dx).start()

    def g_finish():
        for h in range(HALVES):
            full = gown[h]
            for dx in range(1, chips):
                g_x(h, dx).wait_recv()
                full = full + gxr[h, dx - 1].astype(jnp.float32)
            gt[:, h * half : (h + 1) * half] = full.T
        lengths = [len_ref[d] for d in range(docs)]
        owners = [own_ref[d] for d in range(docs)]
        starts, ends, targets = [], [], []
        running = jnp.int32(0)
        for d in range(docs):
            starts.append(running)
            running = running + lengths[d]
            ends.append(running)
            before = jnp.int32(0)
            for e in range(d):
                before = before + jnp.where(owners[e] == owners[d], 1, 0)
            targets.append(owners[d] * slots + before)
        position = z * rows + lax.broadcasted_iota(jnp.int32, (1, rows), 1)
        for o in range(docs):
            start, end = jnp.int32(0), jnp.int32(0)
            for d in range(docs):
                start = jnp.where(targets[d] == o, starts[d], start)
                end = jnp.where(targets[d] == o, ends[d], end)
            inside = (position >= start) & (position < end)
            gm[o * width : (o + 1) * width, :] = jnp.where(inside, gt[...], 0.0).astype(jnp.bfloat16)
        scales = []
        for s in range(slots):
            own_length = jnp.int32(0)
            for d in range(docs):
                own_length = jnp.where(targets[d] == z * slots + s, lengths[d], own_length)
            scales.append(lax.rsqrt(jnp.full((1, cols), own_length, jnp.int32).astype(jnp.float32)))
        return scales

    def i_matmul(u, steps):
        k, r = u // HALVES, u % HALVES
        for j in steps:
            if k == 0:
                a_copy(r, j).wait()
            if r == 0:
                p_copy(k, j).wait()
            term = jnp.dot(
                acts[r * half : (r + 1) * half, j * kin : (j + 1) * kin],
                pin[j * kin : (j + 1) * kin, k * cols : (k + 1) * cols],
                preferred_element_type=jnp.float32,
            )
            for core in range(CORES):
                piece = term[core * half // CORES : (core + 1) * half // CORES]
                if j == 0:
                    ip[u, core] = piece
                else:
                    ip[u, core] += piece

    def i_share(u):
        i_sib(u).wait_recv()
        total = ip[u, c] + ir[u]
        isum[u] = total
        ixs[u] = total.astype(jnp.bfloat16)
        for dx in range(1, chips):
            i_x(u, dx).start()

    def i_merge(u):
        full = isum[u]
        for dx in range(1, chips):
            i_x(u, dx).wait_recv()
            full = full + ixr[u, dx - 1].astype(jnp.float32)
        il[u // HALVES, u % HALVES, c] = full.astype(jnp.bfloat16)
        i_gather(u).start()

    def outer(k):
        for r in range(HALVES):
            i_gather(k * HALVES + r).wait_recv()
        part = jnp.dot(gm[...], il[k].reshape(rows, cols), preferred_element_type=jnp.float32)
        height = slots * width
        for o in range(toks):
            piece = part[o * height : (o + 1) * height]
            zf[k, o] = piece
            zs[k, o] = piece.astype(jnp.bfloat16)
        for dz in sorted(range(1, toks), key=lambda dz: -min(dz, toks - dz)):
            z_copy(k, dz).start()

    def finish(k, scales):
        total = zf[k, z]
        for dz in range(1, toks):
            z_copy(k, dz).wait_recv()
            total = total + zr[k, dz - 1].astype(jnp.float32)
        for s in range(slots):
            res_ref[s, :, k * cols : (k + 1) * cols] = total[s * width : (s + 1) * width] * scales[s]

    split = IN_STEPS // 2
    first, second = range(split), range(split, IN_STEPS)
    g_matmul(0)
    pl.semaphore_wait(barrier, len(peers))
    g_sib(0).start()
    g_matmul(1)
    g_sib(1).start()
    g_share(0)
    i_matmul(0, first)
    g_share(1)
    i_matmul(0, second)
    i_sib(0).start()
    i_matmul(1, first)
    i_share(0)
    i_matmul(1, second)
    i_sib(1).start()
    i_matmul(2, first)
    i_share(1)
    i_matmul(2, second)
    i_sib(2).start()
    i_matmul(3, first)
    i_share(2)
    i_matmul(3, second)
    i_sib(3).start()
    scales = g_finish()
    i_share(3)
    i_merge(0)
    i_merge(1)
    outer(0)
    i_merge(2)
    i_merge(3)
    outer(1)
    for k in range(HALVES):
        finish(k, scales)

    for h in range(HALVES):
        g_sib(h).wait_send()
        for dx in range(1, chips):
            g_x(h, dx).wait_send()
    for u in range(HALVES * HALVES):
        i_sib(u).wait_send()
        i_gather(u).wait_send()
        for dx in range(1, chips):
            i_x(u, dx).wait_send()
    for k in range(HALVES):
        for dz in range(1, toks):
            z_copy(k, dz).wait_send()


def shards(toks, feats, acts, grads, proj_in, proj_out, doc_lengths, doc_owner):
    rows, din = acts.shape
    dout = grads.shape[1]
    rank = proj_in.shape[1]
    docs = doc_lengths.shape[0]
    slots = docs // toks
    chips = feats // CORES
    width = rank // feats
    half, cols = rows // HALVES, rank // HALVES
    units = HALVES * HALVES
    share = half // CORES
    f32, bf16 = jnp.float32, jnp.bfloat16
    vmem, dma = pltpu.VMEM, pltpu.SemaphoreType.DMA
    away, far = chips - 1, toks - 1
    height = slots * width
    return pl.pallas_call(
        functools.partial(kernel, toks, feats),
        out_shape=jax.ShapeDtypeStruct((slots, width, rank), f32),
        in_specs=[pl.BlockSpec(memory_space=pltpu.SMEM)] * 2 + [pl.BlockSpec(memory_space=pl.ANY)] * 4,
        out_specs=pl.BlockSpec(memory_space=pltpu.VMEM),
        scratch_shapes=[
            vmem((rows, din), bf16),
            vmem((rows, dout), bf16),
            vmem((din, rank), bf16),
            vmem((dout, rank), bf16),
            vmem((CORES, HALVES, chips, half, width), f32),
            vmem((HALVES, chips, half, width), f32),
            vmem((HALVES, half, width), f32),
            vmem((HALVES, away, half, width), bf16),
            vmem((HALVES, away, half, width), bf16),
            vmem((width, rows), f32),
            vmem((docs * width, rows), bf16),
            vmem((units, CORES, share, cols), f32),
            vmem((units, share, cols), f32),
            vmem((units, share, cols), f32),
            vmem((units, share, cols), bf16),
            vmem((units, away, share, cols), bf16),
            vmem((HALVES, HALVES, CORES, share, cols), bf16),
            vmem((HALVES, toks, height, cols), f32),
            vmem((HALVES, toks, height, cols), bf16),
            vmem((HALVES, far, height, cols), bf16),
            dma((HALVES, IN_STEPS)),
            dma((OUT_STEPS,)),
            dma((HALVES, IN_STEPS)),
            dma((OUT_STEPS,)),
            dma((HALVES,)),
            dma((HALVES,)),
            dma((HALVES, away)),
            dma((HALVES, away)),
            dma((units,)),
            dma((units,)),
            dma((units, away)),
            dma((units, away)),
            dma((units,)),
            dma((units,)),
            dma((HALVES, far)),
            dma((HALVES, far)),
        ],
        compiler_params=pltpu.CompilerParams(
            collective_id=0, has_side_effects=True, vmem_limit_bytes=62 * 1024 * 1024
        ),
        name="projected_grads",
    )(doc_lengths, doc_owner, acts, grads, proj_in, proj_out)


def solution(mesh):
    in_specs = (
        P(("grp", "tok"), "feat"),
        P(("grp", "tok"), "feat"),
        P("feat", None),
        P("feat", None),
        P("grp"),
        P("grp"),
    )
    out_specs = P(("grp", "tok"), "feat", None)
    body = functools.partial(shards, mesh.shape["tok"], mesh.shape["feat"])
    return jax.shard_map(body, mesh=mesh, in_specs=in_specs, out_specs=out_specs, check_vma=False)
```

```python
import functools
import jax
import jax.numpy as jnp
from jax import lax
from jax.experimental import pallas as pl
from jax.experimental.pallas import tpu as pltpu
from jax.sharding import PartitionSpec as P

MESH = pl.DeviceIdType.MESH
CORES = 2
HALVES = 2
CHUNKS = 4
OUT_STEPS = 2
IN_STEPS = 7
AHEAD = 8


def kernel(
    toks, feats, len_ref, own_ref, acts_hbm, grads_hbm, pin_hbm, pout_hbm, res_ref,
    acts, grads, pin, pout,
    gp, gr, gown, gxs, gxr, gt, gm,
    ip, ir, isum, ixs, ixr, il, zf, zs, zr,
    a_sem, g_sem, pi_sem, po_sem,
    gs_send, gs_recv, gx_send, gx_recv, is_send, is_recv, ix_send, ix_recv,
    ig_send, ig_recv, z_send, z_recv,
):
    z = lax.axis_index("tok")
    f = lax.axis_index("feat")
    chips = feats // CORES
    x, c = f // CORES, lax.rem(f, CORES)
    oc = 1 - c
    sib = {"feat": x * CORES + oc}
    docs = len_ref.shape[0]
    slots = docs // toks
    rows, din = acts.shape
    dout = grads.shape[1]
    half = rows // HALVES
    width = gown.shape[2]
    rank = pin.shape[1]
    cols = rank // CHUNKS
    units = CHUNKS * HALVES
    kin, kout = din // IN_STEPS, dout // OUT_STEPS

    def chip(dx):
        return lax.rem(x + dx, chips)

    def at_x(dx):
        return {"feat": chip(dx) * CORES + c}

    def tok(dz):
        return lax.rem(z + dz, toks)

    def g_copy(h, j):
        return pltpu.make_async_copy(
            grads_hbm.at[pl.ds(h * half, half), pl.ds(j * kout, kout)],
            grads.at[pl.ds(h * half, half), pl.ds(j * kout, kout)],
            g_sem.at[h, j],
        )

    def q_copy(j):
        return pltpu.make_async_copy(
            pout_hbm.at[pl.ds(j * kout, kout)], pout.at[pl.ds(j * kout, kout)], po_sem.at[j]
        )

    def a_copy(r, j):
        return pltpu.make_async_copy(
            acts_hbm.at[pl.ds(r * half, half), pl.ds(j * kin, kin)],
            acts.at[pl.ds(r * half, half), pl.ds(j * kin, kin)],
            a_sem.at[r, j],
        )

    def p_copy(j):
        return pltpu.make_async_copy(
            pin_hbm.at[pl.ds(j * kin, kin)], pin.at[pl.ds(j * kin, kin)], pi_sem.at[j]
        )

    barrier = pltpu.get_barrier_semaphore()
    peers = [sib] + [at_x(dx) for dx in range(1, chips)] + [{"tok": tok(dz)} for dz in range(1, toks)]
    for peer in peers:
        pl.semaphore_signal(barrier, inc=1, device_id=peer, device_id_type=MESH)

    loads = [copy for j in range(OUT_STEPS) for copy in (q_copy(j), g_copy(0, j))]
    loads += [g_copy(h, j) for h in range(1, HALVES) for j in range(OUT_STEPS)]
    loads += [copy for j in range(IN_STEPS) for copy in (p_copy(j), a_copy(0, j))]
    loads += [a_copy(r, j) for r in range(1, HALVES) for j in range(IN_STEPS)]
    issued = [0]

    def issue(count):
        for copy in loads[issued[0] : issued[0] + count]:
            copy.start()
        issued[0] += count

    def arrive(copy):
        copy.wait()
        issue(1)

    issue(AHEAD)

    def remote(src, dst, send, recv, device):
        return pltpu.make_async_remote_copy(
            src_ref=src, dst_ref=dst, send_sem=send, recv_sem=recv, device_id=device, device_id_type=MESH
        )

    def g_sib(h):
        return remote(gp.at[oc, h], gr.at[h], gs_send.at[h], gs_recv.at[h], sib)

    def g_x(h, dx):
        return remote(gxs.at[h, dx - 1], gxr.at[h, dx - 1], gx_send.at[h, dx - 1], gx_recv.at[h, dx - 1], at_x(dx))

    def i_sib(u):
        return remote(ip.at[u, oc], ir.at[u], is_send.at[u], is_recv.at[u], sib)

    def i_x(u, dx):
        return remote(ixs.at[u], ixr.at[u, dx - 1], ix_send.at[u, dx - 1], ix_recv.at[u, dx - 1], at_x(dx))

    def i_gather(u):
        place = il.at[u // HALVES, u % HALVES, c]
        return remote(place, place, ig_send.at[u], ig_recv.at[u], sib)

    def z_copy(k, dz):
        return remote(
            zs.at[k, tok(dz)], zr.at[k, dz - 1], z_send.at[k, dz - 1], z_recv.at[k, dz - 1], {"tok": tok(dz)}
        )

    def g_matmul(h):
        total = None
        for j in range(OUT_STEPS):
            if h == 0:
                arrive(q_copy(j))
            arrive(g_copy(h, j))
            term = jnp.dot(
                grads[h * half : (h + 1) * half, j * kout : (j + 1) * kout],
                pout[j * kout : (j + 1) * kout, :],
                preferred_element_type=jnp.float32,
            )
            total = term if total is None else total + term
        for b in range(feats):
            gp[b % CORES, h, b // CORES] = total[:, b * width : (b + 1) * width]

    def g_share(h):
        g_sib(h).wait_recv()
        gown[h] = gp[c, h, x] + gr[h, x]
        for dx in range(1, chips):
            gxs[h, dx - 1] = (gp[c, h, chip(dx)] + gr[h, chip(dx)]).astype(jnp.bfloat16)
            g_x(h, dx).start()

    def g_finish():
        for h in range(HALVES):
            full = gown[h]
            for dx in range(1, chips):
                g_x(h, dx).wait_recv()
                full = full + gxr[h, dx - 1].astype(jnp.float32)
            gt[:, h * half : (h + 1) * half] = full.T
        lengths = [len_ref[d] for d in range(docs)]
        owners = [own_ref[d] for d in range(docs)]
        starts, ends, targets = [], [], []
        running = jnp.int32(0)
        for d in range(docs):
            starts.append(running)
            running = running + lengths[d]
            ends.append(running)
            before = jnp.int32(0)
            for e in range(d):
                before = before + jnp.where(owners[e] == owners[d], 1, 0)
            targets.append(owners[d] * slots + before)
        position = z * rows + lax.broadcasted_iota(jnp.int32, (1, rows), 1)
        for o in range(docs):
            start, end = jnp.int32(0), jnp.int32(0)
            for d in range(docs):
                start = jnp.where(targets[d] == o, starts[d], start)
                end = jnp.where(targets[d] == o, ends[d], end)
            inside = (position >= start) & (position < end)
            gm[o * width : (o + 1) * width, :] = jnp.where(inside, gt[...], 0.0).astype(jnp.bfloat16)
        scales = []
        for s in range(slots):
            own_length = jnp.int32(0)
            for d in range(docs):
                own_length = jnp.where(targets[d] == z * slots + s, lengths[d], own_length)
            scales.append(lax.rsqrt(jnp.full((1, cols), own_length, jnp.int32).astype(jnp.float32)))
        return scales

    def i_matmul(p, r, steps):
        wide = rank // HALVES
        per = CHUNKS // HALVES
        for j in steps:
            if p == 0:
                if r == 0:
                    arrive(p_copy(j))
                arrive(a_copy(r, j))
            term = jnp.dot(
                acts[r * half : (r + 1) * half, j * kin : (j + 1) * kin],
                pin[j * kin : (j + 1) * kin, p * wide : (p + 1) * wide],
                preferred_element_type=jnp.float32,
            )
            for q in range(per):
                u = (p * per + q) * HALVES + r
                for core in range(CORES):
                    piece = term[core * half // CORES : (core + 1) * half // CORES, q * cols : (q + 1) * cols]
                    if j == 0:
                        ip[u, core] = piece
                    else:
                        ip[u, core] += piece
        if steps[-1] == IN_STEPS - 1:
            for q in range(per):
                i_sib((p * per + q) * HALVES + r).start()

    def i_share(u):
        i_sib(u).wait_recv()
        total = ip[u, c] + ir[u]
        isum[u] = total
        ixs[u] = total.astype(jnp.bfloat16)
        for dx in range(1, chips):
            i_x(u, dx).start()

    def i_merge(u):
        full = isum[u]
        for dx in range(1, chips):
            i_x(u, dx).wait_recv()
            full = full + ixr[u, dx - 1].astype(jnp.float32)
        il[u // HALVES, u % HALVES, c] = full.astype(jnp.bfloat16)
        i_gather(u).start()

    def outer(k):
        for r in range(HALVES):
            i_gather(k * HALVES + r).wait_recv()
        part = jnp.dot(gm[...], il[k].reshape(rows, cols), preferred_element_type=jnp.float32)
        height = slots * width
        for o in range(toks):
            piece = part[o * height : (o + 1) * height]
            zf[k, o] = piece
            zs[k, o] = piece.astype(jnp.bfloat16)
        for dz in sorted(range(1, toks), key=lambda dz: -min(dz, toks - dz)):
            z_copy(k, dz).start()

    def finish(k, scales):
        total = zf[k, z]
        for dz in range(1, toks):
            z_copy(k, dz).wait_recv()
            total = total + zr[k, dz - 1].astype(jnp.float32)
        for s in range(slots):
            res_ref[s, :, k * cols : (k + 1) * cols] = total[s * width : (s + 1) * width] * scales[s]

    split = IN_STEPS // 2
    first, second = range(split), range(split, IN_STEPS)
    g_matmul(0)
    pl.semaphore_wait(barrier, len(peers))
    g_sib(0).start()
    g_matmul(1)
    g_sib(1).start()
    g_share(0)
    i_matmul(0, 0, first)
    g_share(1)
    i_matmul(0, 0, second)
    i_matmul(0, 1, first)
    i_share(0)
    i_matmul(0, 1, second)
    i_matmul(1, 0, first)
    i_share(1)
    i_share(2)
    i_share(3)
    i_matmul(1, 0, second)
    i_matmul(1, 1, first)
    i_share(4)
    i_matmul(1, 1, second)
    scales = g_finish()
    i_merge(0)
    i_merge(1)
    i_share(5)
    i_share(6)
    i_share(7)
    outer(0)
    i_merge(2)
    i_merge(3)
    outer(1)
    i_merge(4)
    i_merge(5)
    outer(2)
    i_merge(6)
    i_merge(7)
    outer(3)
    for k in range(CHUNKS):
        finish(k, scales)

    for h in range(HALVES):
        g_sib(h).wait_send()
        for dx in range(1, chips):
            g_x(h, dx).wait_send()
    for u in range(units):
        i_sib(u).wait_send()
        i_gather(u).wait_send()
        for dx in range(1, chips):
            i_x(u, dx).wait_send()
    for k in range(CHUNKS):
        for dz in range(1, toks):
            z_copy(k, dz).wait_send()


def shards(toks, feats, acts, grads, proj_in, proj_out, doc_lengths, doc_owner):
    rows, din = acts.shape
    dout = grads.shape[1]
    rank = proj_in.shape[1]
    docs = doc_lengths.shape[0]
    slots = docs // toks
    chips = feats // CORES
    width = rank // feats
    half, cols = rows // HALVES, rank // CHUNKS
    units = CHUNKS * HALVES
    share = half // CORES
    f32, bf16 = jnp.float32, jnp.bfloat16
    vmem, dma = pltpu.VMEM, pltpu.SemaphoreType.DMA
    away, far = chips - 1, toks - 1
    height = slots * width
    return pl.pallas_call(
        functools.partial(kernel, toks, feats),
        out_shape=jax.ShapeDtypeStruct((slots, width, rank), f32),
        in_specs=[pl.BlockSpec(memory_space=pltpu.SMEM)] * 2 + [pl.BlockSpec(memory_space=pl.ANY)] * 4,
        out_specs=pl.BlockSpec(memory_space=pltpu.VMEM),
        scratch_shapes=[
            vmem((rows, din), bf16),
            vmem((rows, dout), bf16),
            vmem((din, rank), bf16),
            vmem((dout, rank), bf16),
            vmem((CORES, HALVES, chips, half, width), f32),
            vmem((HALVES, chips, half, width), f32),
            vmem((HALVES, half, width), f32),
            vmem((HALVES, away, half, width), bf16),
            vmem((HALVES, away, half, width), bf16),
            vmem((width, rows), f32),
            vmem((docs * width, rows), bf16),
            vmem((units, CORES, share, cols), f32),
            vmem((units, share, cols), f32),
            vmem((units, share, cols), f32),
            vmem((units, share, cols), bf16),
            vmem((units, away, share, cols), bf16),
            vmem((CHUNKS, HALVES, CORES, share, cols), bf16),
            vmem((CHUNKS, toks, height, cols), f32),
            vmem((CHUNKS, toks, height, cols), bf16),
            vmem((CHUNKS, far, height, cols), bf16),
            dma((HALVES, IN_STEPS)),
            dma((HALVES, OUT_STEPS)),
            dma((IN_STEPS,)),
            dma((OUT_STEPS,)),
            dma((HALVES,)),
            dma((HALVES,)),
            dma((HALVES, away)),
            dma((HALVES, away)),
            dma((units,)),
            dma((units,)),
            dma((units, away)),
            dma((units, away)),
            dma((units,)),
            dma((units,)),
            dma((CHUNKS, far)),
            dma((CHUNKS, far)),
        ],
        compiler_params=pltpu.CompilerParams(
            collective_id=0, has_side_effects=True, vmem_limit_bytes=62 * 1024 * 1024
        ),
        name="projected_grads",
    )(doc_lengths, doc_owner, acts, grads, proj_in, proj_out)


def solution(mesh):
    in_specs = (
        P(("grp", "tok"), "feat"),
        P(("grp", "tok"), "feat"),
        P("feat", None),
        P("feat", None),
        P("grp"),
        P("grp"),
    )
    out_specs = P(("grp", "tok"), "feat", None)
    body = functools.partial(shards, mesh.shape["tok"], mesh.shape["feat"])
    return jax.shard_map(body, mesh=mesh, in_specs=in_specs, out_specs=out_specs, check_vma=False)
```
